32 devices in a mesh: tm: 16 (over z, y, core), space: 2 (over x).
Axes of the slice: x: 2, y: 2, z: 4, core: 2. Of those that a mesh axis runs over, the one named last changes fastest.
Arguments:
- iterate: float32 [16, 4, 128, 64, 128], P('tm', None, 'space'), may hold values from -6 to 6
- right_side: float32 [16, 4, 128, 64, 128], P('tm', None, 'space'), may hold values from -6 to 6
- diffusivity: float32 [128, 64, 128], P('space'), may hold values from 0.5 to 2
- velocity: float32 [3], replicated, may hold values from -2 to 2
Outputs:
- next_iterate: float32 [16, 4, 128, 64, 128], P('tm', None, 'space')
The draws below stay inside these ranges and needn't reach their ends.
All inputs are finite; a program needn't handle non-finite values.
Results may differ from the reference program's by a relative error of at most 0.0003.
Values sent between devices are 32-bit elements; how exact they have to be, the bound alone decides.
A program may use at most 192 MiB of HBM per device.

```python
import math
import jax
import jax.numpy as jnp
from jax import lax

NX = 128
NY = 128
NZ = 64
NODES = 4
STEPS = 16


def draw_right_side(key, part):
    rough_key = jax.random.fold_in(jax.random.fold_in(key, 17), 0)
    rough = jax.random.truncated_normal(rough_key, -6.0, 6.0, (STEPS, NODES, NX, NZ, NY), jnp.float32)
    return rough


def block_levels(key, extent, pieces, least, largest):
    def one(axis_at, shards_of):
        steps = jax.random.uniform(jax.random.fold_in(jax.random.fold_in(key, 6), axis_at), (shards_of,), jnp.float32, least / len(pieces), largest / len(pieces))
        return jnp.repeat(jnp.exp(steps), extent[axis_at] // shards_of).reshape((-1,) + (1,) * (len(extent) - axis_at - 1))

    factor_of = one(*pieces[0])
    for cut in pieces[1:]:
        factor_of = factor_of * one(*cut)
    return factor_of


def centred(own_key, shape, spread, limit, pieces=(), kind=jnp.bfloat16):
    level = block_levels(own_key, shape, pieces, -0.22, 0.18) if pieces else 1.0
    values = jax.random.normal(own_key, shape, jnp.float32) * spread * level
    return jnp.minimum(jnp.maximum(values, -limit), limit).astype(kind)


def setup_inputs(seed: int = 0) -> dict:
    streams_of = jax.random.split(jax.random.key(seed), 5)
    return {
        "iterate": centred(streams_of[0], (STEPS, NODES, NX, NZ, NY), 1.0, 6.0, ((0, 16), (2, 2)), jnp.float32),
        "right_side": draw_right_side(jax.random.fold_in(streams_of[4], 71), 0),
        "diffusivity": jnp.clip(jnp.exp(math.log(2.0) - 1.3862944 * jax.random.uniform(streams_of[2], (NX, NZ, NY), jnp.float32) ** block_levels(streams_of[2], (NX, NZ, NY), ((0, 2),), -0.2, 0.2)), 0.5, 2.0),
        "velocity": jnp.clip(jax.random.uniform(streams_of[3], (3,), jnp.float32, -2.0, 2.0), -2.0, 2.0),
    }


diffusion_number = 16.0
circulant_alpha = 0.1


def collocation_matrix():
    radau_nodes = [0.088587959512703947, 0.40946686444073471, 0.78765946176084706, 1.0]
    matrix = [[0.0] * 4 for row_index in range(4)]
    for column_index in range(4):
        coefficients = [1.0]
        for other_index in range(4):
            if other_index != column_index:
                scale_value = 1.0 / (radau_nodes[column_index] - radau_nodes[other_index])
                shifted = [0.0] + [value * scale_value for value in coefficients]
                lowered = [-radau_nodes[other_index] * scale_value * value for value in coefficients] + [0.0]
                coefficients = [left_value + right_value for left_value, right_value in zip(shifted, lowered)]
        for row_index in range(4):
            total = 0.0
            for power_index in range(len(coefficients)):
                total = total + coefficients[power_index] * radau_nodes[row_index] ** (power_index + 1) / (power_index + 1)
            matrix[row_index][column_index] = total
    return matrix


def solve_system(matrix, target):
    count = len(target)
    rows_list = [list(matrix[row_index]) + [target[row_index]] for row_index in range(count)]
    for column in range(count):
        best_row = column
        for candidate in range(column + 1, count):
            if abs(rows_list[candidate][column]) > abs(rows_list[best_row][column]):
                best_row = candidate
        saved_row = rows_list[column]
        rows_list[column] = rows_list[best_row]
        rows_list[best_row] = saved_row
        leader = rows_list[column][column]
        for other_row in range(count):
            if other_row != column:
                factor = rows_list[other_row][column] / leader
                rows_list[other_row] = [left_value - factor * right_value for left_value, right_value in zip(rows_list[other_row], rows_list[column])]
    return [rows_list[row_index][count] / rows_list[row_index][row_index] for row_index in range(count)]


def node_basis():
    matrix = collocation_matrix()
    helper = [[0.0] * 4 for row_index in range(4)]
    coefficients = [0.0, 0.0, 0.0, 0.0, 1.0]
    for order in range(1, 5):
        product = [[sum(matrix[row_index][inner] * helper[inner][column] for inner in range(4)) for column in range(4)] for row_index in range(4)]
        for row_index in range(4):
            product[row_index][row_index] = product[row_index][row_index] + coefficients[5 - order]
        helper = product
        trace_value = sum(sum(matrix[row_index][inner] * helper[inner][row_index] for inner in range(4)) for row_index in range(4))
        coefficients[4 - order] = -trace_value / order
    roots_list = [(0.4 + 0.9j) ** power_index for power_index in range(4)]
    for sweep in range(400):
        for root_index in range(4):
            current = roots_list[root_index]
            numer = 0.0
            for power_index in range(4, -1, -1):
                numer = numer * current + coefficients[power_index]
            denom = 1.0
            for other_index in range(4):
                if other_index != root_index:
                    denom = denom * (current - roots_list[other_index])
            roots_list[root_index] = current - numer / denom
    vectors = [[0.0] * 4 for row_index in range(4)]
    for root_index in range(4):
        shifted = [[matrix[row_index][column] - (roots_list[root_index] if row_index == column else 0.0) for column in range(3)] for row_index in range(3)]
        target = [-matrix[row_index][3] for row_index in range(3)]
        parts = solve_system(shifted, target) + [1.0 + 0.0j]
        for row_index in range(4):
            vectors[row_index][root_index] = parts[row_index]
    inverse = [[0.0] * 4 for row_index in range(4)]
    for column in range(4):
        unit = [1.0 if row_index == column else 0.0 for row_index in range(4)]
        parts = solve_system(vectors, unit)
        for row_index in range(4):
            inverse[row_index][column] = parts[row_index]
    weights = [sum(inverse[row_index][column] for column in range(4)) for row_index in range(4)]
    return roots_list, vectors, inverse, weights


def complex_vector(numbers):
    real_values = jnp.asarray([complex(value).real for value in numbers], jnp.float32)
    imag_values = jnp.asarray([complex(value).imag for value in numbers], jnp.float32)
    return real_values + 1j * imag_values


def complex_matrix(numbers):
    real_values = jnp.asarray([[complex(value).real for value in row] for row in numbers], jnp.float32)
    imag_values = jnp.asarray([[complex(value).imag for value in row] for row in numbers], jnp.float32)
    return real_values + 1j * imag_values


def spatial_operator(field_values, diffusivity, velocity):
    upper_x = jnp.roll(field_values, -1, axis=2)
    lower_x = jnp.roll(field_values, 1, axis=2)
    upper_z = jnp.roll(field_values, -1, axis=3)
    lower_z = jnp.roll(field_values, 1, axis=3)
    upper_y = jnp.roll(field_values, -1, axis=4)
    lower_y = jnp.roll(field_values, 1, axis=4)
    laplace = (upper_x + lower_x) + (upper_z + lower_z) + (upper_y + lower_y) - 6.0 * field_values
    transport = velocity[0] * (upper_x - lower_x) + velocity[1] * (upper_y - lower_y) + velocity[2] * (upper_z - lower_z)
    return diffusion_number * diffusivity * laplace - 0.5 * transport


def reference(iterate, right_side, diffusivity, velocity):
    collocation = jnp.asarray(collocation_matrix(), jnp.float32)
    applied = spatial_operator(iterate, diffusivity, velocity)
    coupled = jnp.einsum("mn,snxzy->smxzy", collocation, applied, precision=lax.Precision.HIGHEST)
    previous = jnp.concatenate([jnp.zeros_like(iterate[:1, 3]), iterate[:-1, 3]], axis=0)
    residual = right_side - iterate + coupled + previous[:, None]
    gamma_base = circulant_alpha ** (1.0 / STEPS)
    step_power = jnp.arange(STEPS, dtype=jnp.int32).astype(jnp.float32)
    step_scale = jnp.power(jnp.float32(gamma_base), step_power)
    spectrum = jnp.fft.rfftn(residual * step_scale[:, None, None, None, None], axes=(0, 2, 3, 4))
    theta_x = jnp.arange(NX, dtype=jnp.int32).astype(jnp.float32) * (2.0 * math.pi / NX)
    theta_z = jnp.arange(NZ, dtype=jnp.int32).astype(jnp.float32) * (2.0 * math.pi / NZ)
    theta_y = jnp.arange(NY // 2 + 1, dtype=jnp.int32).astype(jnp.float32) * (2.0 * math.pi / NY)
    symbol_real = diffusion_number * ((2.0 * jnp.cos(theta_x)[:, None, None] - 2.0) + (2.0 * jnp.cos(theta_z)[None, :, None] - 2.0) + (2.0 * jnp.cos(theta_y)[None, None, :] - 2.0))
    symbol_imag = -(velocity[0] * jnp.sin(theta_x)[:, None, None] + velocity[1] * jnp.sin(theta_y)[None, None, :] + velocity[2] * jnp.sin(theta_z)[None, :, None])
    symbol = symbol_real + 1j * symbol_imag
    values, vectors, inverse, weights = node_basis()
    eigen = complex_vector(values)
    basis = complex_matrix(vectors)
    basis_inverse = complex_matrix(inverse)
    ones_weights = complex_vector(weights)
    damping = 1.0 / (1.0 - eigen[:, None, None, None] * symbol[None])
    ones_image = jnp.einsum("pm,mxzy->pxzy", basis, ones_weights[:, None, None, None] * damping, precision=lax.Precision.HIGHEST)
    phases = jnp.arange(STEPS, dtype=jnp.int32).astype(jnp.float32) * (2.0 * math.pi / STEPS)
    shift_factors = gamma_base * (jnp.cos(phases) - 1j * jnp.sin(phases))

    def solve_one(operands):
        block, shift_factor = operands
        inner = jnp.einsum("mn,nxzy->mxzy", basis_inverse, block, precision=lax.Precision.HIGHEST) * damping
        image = jnp.einsum("pm,mxzy->pxzy", basis, inner, precision=lax.Precision.HIGHEST)
        factor = shift_factor * image[3] / (1.0 - shift_factor * ones_image[3])
        return image + ones_image * factor[None]

    solved = lax.map(solve_one, (spectrum, shift_factors))
    correction = jnp.fft.irfftn(solved, s=(STEPS, NX, NZ, NY), axes=(0, 2, 3, 4))
    unscale = jnp.power(jnp.float32(gamma_base), -step_power)
    return iterate + correction * unscale[:, None, None, None, None]
```

```python
import math

import jax
import jax.numpy as jnp
from jax import lax
from jax.sharding import PartitionSpec as P

diffusion_number = 16.0
circulant_alpha = 0.1


def padded_2(block, sides, width):
    for axis, dim in sides:
        count = lax.axis_size(axis)
        forward = [(i, i + 1) for i in range(count - 1)]
        forward.append((count - 1, 0))
        backward = [(target, source) for source, target in forward]
        low = lax.ppermute(
            lax.slice_in_dim(block, block.shape[dim] - width, None, axis=dim), axis, forward
        )
        high = lax.ppermute(lax.slice_in_dim(block, 0, width, axis=dim), axis, backward)
        block = jnp.concatenate([low, block, high], axis=dim)
    return block


def passed_along(value, axis, steps):
    count = lax.axis_size(axis)
    leading, last = (max(0, -steps), min(count, count - steps))
    return lax.ppermute(value, axis, [(source, source + steps) for source in range(leading, last)])


def collocation_matrix():
    radau_nodes = [0.08858795951270394, 0.4094668644407347, 0.7876594617608471, 1.0]
    matrix = [[0.0] * 4 for row_index in range(4)]
    for column_index in range(4):
        coefficients = [1.0]
        for other_index in range(4):
            if other_index != column_index:
                scale_value = 1.0 / (radau_nodes[column_index] - radau_nodes[other_index])
                shifted = [0.0] + [value * scale_value for value in coefficients]
                lowered = [
                    -radau_nodes[other_index] * scale_value * value for value in coefficients
                ] + [0.0]
                coefficients = [
                    left_value + right_value for left_value, right_value in zip(shifted, lowered)
                ]
        for row_index in range(4):
            total = 0.0
            for power_index in range(len(coefficients)):
                total = total + coefficients[power_index] * radau_nodes[row_index] ** (
                    power_index + 1
                ) / (power_index + 1)
            matrix[row_index][column_index] = total
    return matrix


def solve_system(matrix, target):
    count = len(target)
    rows_list = [list(matrix[row_index]) + [target[row_index]] for row_index in range(count)]
    for column in range(count):
        best_row = column
        for candidate in range(column + 1, count):
            if abs(rows_list[candidate][column]) > abs(rows_list[best_row][column]):
                best_row = candidate
        saved_row = rows_list[column]
        rows_list[column] = rows_list[best_row]
        rows_list[best_row] = saved_row
        leader = rows_list[column][column]
        for other_row in range(count):
            if other_row != column:
                factor = rows_list[other_row][column] / leader
                rows_list[other_row] = [
                    left_value - factor * right_value
                    for left_value, right_value in zip(rows_list[other_row], rows_list[column])
                ]
    return [
        rows_list[row_index][count] / rows_list[row_index][row_index] for row_index in range(count)
    ]


def node_basis():
    matrix = collocation_matrix()
    helper = [[0.0] * 4 for row_index in range(4)]
    coefficients = [0.0, 0.0, 0.0, 0.0, 1.0]
    for order in range(1, 5):
        product = [
            [
                sum((matrix[row_index][inner] * helper[inner][column] for inner in range(4)))
                for column in range(4)
            ]
            for row_index in range(4)
        ]
        for row_index in range(4):
            product[row_index][row_index] = product[row_index][row_index] + coefficients[5 - order]
        helper = product
        trace_value = sum(
            (
                sum((matrix[row_index][inner] * helper[inner][row_index] for inner in range(4)))
                for row_index in range(4)
            )
        )
        coefficients[4 - order] = -trace_value / order
    roots_list = [(0.4 + 0.9j) ** power_index for power_index in range(4)]
    for sweep in range(400):
        for root_index in range(4):
            current = roots_list[root_index]
            numer = 0.0
            for power_index in range(4, -1, -1):
                numer = numer * current + coefficients[power_index]
            denom = 1.0
            for other_index in range(4):
                if other_index != root_index:
                    denom = denom * (current - roots_list[other_index])
            roots_list[root_index] = current - numer / denom
    vectors = [[0.0] * 4 for row_index in range(4)]
    for root_index in range(4):
        shifted = [
            [
                matrix[row_index][column] - (roots_list[root_index] if row_index == column else 0.0)
                for column in range(3)
            ]
            for row_index in range(3)
        ]
        target = [-matrix[row_index][3] for row_index in range(3)]
        parts = solve_system(shifted, target) + [1.0 + 0j]
        for row_index in range(4):
            vectors[row_index][root_index] = parts[row_index]
    inverse = [[0.0] * 4 for row_index in range(4)]
    for column in range(4):
        unit = [1.0 if row_index == column else 0.0 for row_index in range(4)]
        parts = solve_system(vectors, unit)
        for row_index in range(4):
            inverse[row_index][column] = parts[row_index]
    weights = [sum((inverse[row_index][column] for column in range(4))) for row_index in range(4)]
    return (roots_list, vectors, inverse, weights)


def exact(subscripts, left, right):
    return jnp.einsum(subscripts, left, right, precision=lax.Precision.HIGH)


def waves(rows, columns, length):
    phases = rows[:, None] * columns[None, :] % length
    angles = phases.astype(jnp.float32) * (2.0 * math.pi / length)
    return jnp.cos(angles), jnp.sin(angles)


def counted(length):
    return jnp.arange(length, dtype=jnp.int32)


def paired_frequency(index, length):
    pair = index // 2
    upper = jnp.where(pair == 0, length // 2, length - pair)
    return jnp.where(index % 2 == 0, pair, upper)


def y_basis(length):
    half = length // 2
    cosine, sine = waves(counted(half), counted(length), length)
    alternating = 1.0 - 2.0 * (counted(length) % 2).astype(jnp.float32)
    imag = jnp.where(counted(half)[:, None] == 0, alternating[None, :], -sine)
    return cosine, imag


def spatial_operator(padded, diffusivity, velocity):
    center = padded[:, 1:-1]
    upper_x = padded[:, 2:]
    lower_x = padded[:, :-2]
    upper_z = jnp.roll(center, -1, axis=2)
    lower_z = jnp.roll(center, 1, axis=2)
    upper_y = jnp.roll(center, -1, axis=3)
    lower_y = jnp.roll(center, 1, axis=3)
    laplace = upper_x + lower_x + (upper_z + lower_z) + (upper_y + lower_y) - 6.0 * center
    transport = (
        velocity[0] * (upper_x - lower_x)
        + velocity[1] * (upper_y - lower_y)
        + velocity[2] * (upper_z - lower_z)
    )
    return diffusion_number * diffusivity * laplace - 0.5 * transport


def damping(wave_x, wave_z, wave_y, sizes, velocity, values):
    real = 0.0
    imag = 0.0
    for wave, size, speed in zip((wave_x, wave_z, wave_y), sizes, (0, 2, 1)):
        theta = wave.astype(jnp.float32) * (2.0 * math.pi / size)
        real = real + diffusion_number * (2.0 * jnp.cos(theta) - 2.0)
        imag = imag - velocity[speed] * jnp.sin(theta)
    damped = []
    for value in values:
        value = complex(value)
        lower_real = 1.0 - (real * value.real - imag * value.imag)
        lower_imag = -(real * value.imag + imag * value.real)
        scale = 1.0 / (lower_real * lower_real + lower_imag * lower_imag)
        damped.append((lower_real * scale, -lower_imag * scale))
    return damped


def times(left, right):
    return (left[0] * right[0] - left[1] * right[1], left[0] * right[1] + left[1] * right[0])


def plus(left, right):
    return (left[0] + right[0], left[1] + right[1])


def mixed(coefficients, terms):
    total = None
    for coefficient, term in zip(coefficients, terms):
        coefficient = complex(coefficient)
        product = times((coefficient.real, coefficient.imag), term)
        total = product if total is None else plus(total, product)
    return total


def swept(arrived, growth, count):
    fields = [(arrived[step, 0], arrived[step, 1]) for step in range(count)]
    total = fields[0]
    power = growth
    for step in range(1, count):
        total = plus(fields[step], times(growth, total))
        power = times(growth, power)
    lower = (1.0 - circulant_alpha * power[0], -circulant_alpha * power[1])
    scale = circulant_alpha / (lower[0] * lower[0] + lower[1] * lower[1])
    current = times(total, (lower[0] * scale, -lower[1] * scale))
    before = []
    for step in range(count):
        before.append(jnp.stack(current))
        current = plus(fields[step], times(growth, current))
    return jnp.stack(before)


def shards(iterate, right_side, diffusivity, velocity):
    steps = lax.axis_size("tm")
    slabs = lax.axis_size("space")
    step = lax.axis_index("tm")
    slab = lax.axis_index("space")
    nodes, x_here, size_z, size_y = iterate.shape[1:]
    size_x = x_here * slabs
    z_here = size_z // slabs
    half = size_y // 2
    sizes = (size_x, size_z, size_y)
    values, vectors, inverse, weights = node_basis()

    previous = passed_along(iterate[:, 3], "tm", 1)
    padded = padded_2(iterate, (("space", 2),), 1)
    applied = spatial_operator(padded[0], diffusivity, velocity)
    matrix = collocation_matrix()
    coupled = jnp.stack(
        [
            sum(float(matrix[row][column]) * applied[column] for column in range(nodes))
            for row in range(nodes)
        ]
    )
    residual = right_side[0] - iterate[0] + coupled + previous

    z_order = paired_frequency(counted(size_z), size_z)
    z_tables = jnp.stack(waves(z_order, counted(size_z), size_z))
    y_real, y_imag = y_basis(size_y)
    y_forward = jnp.stack(
        (jnp.concatenate((y_real, y_imag)).T, jnp.concatenate((y_imag, -y_real)).T)
    )
    along_z = exact("ekz,nxzy->nxeky", z_tables, residual)
    spectrum = exact("nxeky,eyq->nxkq", along_z, y_forward)
    spectrum = lax.all_to_all(spectrum, "space", split_axis=2, concat_axis=1, tiled=True)

    x_cos, x_sin = waves(counted(size_x), counted(size_x), size_x)
    parts = exact("nxzq,xek->enqzk", spectrum, jnp.stack((x_cos, x_sin), axis=1))
    cos_part, sin_part = parts[0], parts[1]
    main_real = cos_part[:, :half] + sin_part[:, half:]
    main_imag = cos_part[:, half:] - sin_part[:, :half]

    def reflected(field):
        pairs = field.reshape(nodes, z_here // 2, 2, size_x)
        fixed = (counted(z_here // 2)[:, None, None] == 0) & (slab == 0)
        return jnp.where(fixed, pairs, pairs[:, :, ::-1]).reshape(field.shape)

    mirror_real = reflected(cos_part[:, 0] - sin_part[:, half])
    mirror_imag = reflected(cos_part[:, half] + sin_part[:, 0])
    low_real = 0.5 * (main_real[:, 0] + mirror_real)
    low_imag = 0.5 * (main_imag[:, 0] - mirror_imag)
    top_real = 0.5 * (main_imag[:, 0] + mirror_imag)
    top_imag = 0.5 * (mirror_real - main_real[:, 0])
    real = jnp.concatenate((low_real[:, None], main_real[:, 1:], top_real[:, None]), axis=1)
    imag = jnp.concatenate((low_imag[:, None], main_imag[:, 1:], top_imag[:, None]), axis=1)

    damped = damping(
        counted(size_x)[None, None, :],
        paired_frequency(slab * z_here + counted(z_here), size_z)[None, :, None],
        counted(half + 1)[:, None, None],
        sizes,
        velocity,
        values,
    )
    targets = [(real[node], imag[node]) for node in range(nodes)]
    inner = [times(damped[node], mixed(inverse[node], targets)) for node in range(nodes)]
    last = jnp.stack(mixed(vectors[3], inner))

    y_each = half // steps
    z_each = -(-z_here // steps)
    rows = y_each * z_here
    spare = z_each * steps - z_here
    main = last[:, :half].reshape(2, steps, rows, size_x)
    top = jnp.pad(last[:, half], ((0, 0), (0, spare), (0, 0))).reshape(2, steps, z_each, size_x)
    sent = jnp.swapaxes(jnp.concatenate((main, top), axis=2), 0, 1)
    arrived = lax.all_to_all(sent, "tm", split_axis=0, concat_axis=0, tiled=True)
    row_y = jnp.concatenate(
        (step * y_each + counted(rows) // z_here, jnp.full((z_each,), half, jnp.int32))
    )
    row_z = jnp.concatenate((counted(rows) % z_here, step * z_each + counted(z_each)))
    row_damped = damping(
        counted(size_x)[None, :],
        paired_frequency(slab * z_here + row_z, size_z)[:, None],
        row_y[:, None],
        sizes,
        velocity,
        values,
    )
    joint = [complex(vectors[3][node]) * complex(weights[node]) for node in range(nodes)]
    growth = mixed(joint, row_damped)
    before = swept(arrived, growth, steps)
    before = lax.all_to_all(before, "tm", split_axis=0, concat_axis=0, tiled=True)
    before = jnp.swapaxes(before, 0, 1)
    before_main = before[:, :, :rows].reshape(2, half, z_here, size_x)
    before_top = before[:, :, rows:].reshape(2, 1, z_each * steps, size_x)[:, :, :z_here]
    before = jnp.concatenate((before_main, before_top), axis=1)

    driven = []
    for node in range(nodes):
        weight = complex(weights[node])
        pushed = times(damped[node], times((weight.real, weight.imag), (before[0], before[1])))
        driven.append(plus(inner[node], pushed))
    packed = []
    for node in range(nodes):
        out_real, out_imag = mixed(vectors[node], driven)
        first_real = out_real[:1] - out_imag[half:]
        first_imag = out_imag[:1] + out_real[half:]
        packed.append(
            jnp.concatenate(
                (
                    jnp.concatenate((first_real, out_real[1:half])),
                    jnp.concatenate((first_imag, out_imag[1:half])),
                ),
                axis=-1,
            )
        )
    solved = jnp.stack(packed)
    x_inverse = jnp.concatenate(
        (jnp.stack((x_cos, x_sin), axis=1), jnp.stack((-x_sin, x_cos), axis=1))
    )
    solved = exact("nqzk,kdx->nxzdq", solved, x_inverse)
    solved = solved.reshape(nodes, size_x, z_here, size_y)
    solved = lax.all_to_all(solved, "space", split_axis=1, concat_axis=2, tiled=True)

    weight = jnp.where(counted(half) == 0, 1.0, 2.0) / (size_x * size_y * size_z)
    back_real, back_imag = (y_real * weight[:, None], y_imag * weight[:, None])
    y_inverse = jnp.stack(
        (jnp.concatenate((back_real, back_imag)), jnp.concatenate((back_imag, -back_real)))
    )
    along_z = exact("ekz,nxkq->nxezq", z_tables, solved)
    correction = exact("nxezq,eqy->nxzy", along_z, y_inverse)
    return iterate + correction[None]


def solution(mesh):
    placed = (
        P("tm", None, "space", None, None),
        P("tm", None, "space", None, None),
        P("space", None, None),
        P(),
    )
    return jax.shard_map(
        shards,
        mesh=mesh,
        in_specs=placed,
        out_specs=P("tm", None, "space", None, None),
        check_vma=False,
    )
```
